32 devices in a mesh: row: 2 (over x), col: 16 (over z, y, core).
Axes of the slice: x: 2, y: 2, z: 4, core: 2. Of those that a mesh axis runs over, the one named last changes fastest.
Arguments:
- hessian_old: float32 [2048, 12288], P('row', 'col'), may hold values from -6 to 6
- gate_rows: bfloat16 [512, 2048], P('col', 'row'), may hold values from -9 to 9
- up_rows: bfloat16 [512, 2048], P('col', 'row'), may hold values from -15 to 15
- gate_columns: bfloat16 [512, 12288], P('row', 'col'), may hold values from -9 to 9
- up_columns: bfloat16 [512, 12288], P('row', 'col'), may hold values from -15 to 15
Outputs:
- hessian_new: float32 [2048, 12288], P('row', 'col')
The draws below stay inside these ranges and needn't reach their ends.
All inputs are finite; a program needn't handle non-finite values.
Results may differ from the reference program's by a relative error of at most 0.00099.
Values may be sent and summed in bfloat16 or wider, within the bound.
A program may use at most 64 MiB of HBM per device.

```python
import jax
import jax.numpy as jnp
from jax import lax

TOKENS = 512
ROWS = 2048
COLS = 12288


def block_scale(key, shape, split, low, high):
    def one(axis_at, shards_of):
        heights = jax.random.uniform(jax.random.fold_in(jax.random.fold_in(key, 6), axis_at), (shards_of,), jnp.float32, low / len(split), high / len(split))
        return jnp.repeat(jnp.exp(heights), shape[axis_at] // shards_of).reshape((-1,) + (1,) * (len(shape) - axis_at - 1))

    level = one(*split[0])
    for cut in split[1:]:
        level = level * one(*cut)
    return level


def gaussian(key, shape, spread, bound, split=(), held_as=jnp.bfloat16):
    loudness = block_scale(key, shape, split, -0.22, 0.18) if split else 1.0
    array = jax.random.normal(key, shape, jnp.float32) * spread * loudness
    return jnp.minimum(jnp.maximum(array, -bound), bound).astype(held_as)


def setup_inputs(seed: int = 0) -> dict:
    splits = jax.random.split(jax.random.key(seed), 6)
    hessian_old = gaussian(splits[0], (ROWS, COLS), 1.0, 6.0, ((0, 2), (1, 16)), jnp.float32)
    gate_rows = gaussian(splits[1], (TOKENS, ROWS), 1.5, 9.0, ((0, 16), (1, 2)))
    up_rows = gaussian(splits[2], (TOKENS, ROWS), 2.5, 15.0, ((0, 16), (1, 2)))
    gate_columns = gaussian(splits[3], (TOKENS, COLS), 1.5, 9.0, ((0, 2), (1, 16)))
    up_columns = gaussian(splits[4], (TOKENS, COLS), 2.5, 15.0, ((0, 2), (1, 16)))
    return dict(hessian_old=hessian_old, gate_rows=gate_rows, up_rows=up_rows, gate_columns=gate_columns, up_columns=up_columns)


def silu_product(gate, up):
    return (jax.nn.silu(gate.astype(jnp.float32)) * up.astype(jnp.float32)).astype(jnp.bfloat16)


def reference(hessian_old, gate_rows, up_rows, gate_columns, up_columns):
    row_inputs = silu_product(gate_rows, up_rows)
    column_inputs = silu_product(gate_columns, up_columns)
    product = lax.dot_general(row_inputs, column_inputs, (((0,), (0,)), ((), ())), preferred_element_type=jnp.float32)
    return 0.5 * hessian_old + product / TOKENS
```

```python
import functools

import jax
import jax.numpy as jnp
from jax import lax
from jax.experimental import pallas as pl
from jax.experimental.pallas import tpu as pltpu
from jax.sharding import PartitionSpec as P

MESH = pl.DeviceIdType.MESH
LIMIT = 40 * 1024 * 1024
FAR = 3
LAG = 2


def silu_product(gate, up):
    return (jax.nn.silu(gate.astype(jnp.float32)) * up.astype(jnp.float32)).astype(jnp.bfloat16)


def update(old, left, right):
    tokens = left.shape[1]
    total = jnp.dot(left, right, preferred_element_type=jnp.float32)
    total = total * (1.0 / tokens) if tokens & (tokens - 1) == 0 else total / tokens
    return 0.5 * old + total


def gather_kernel(dims, old_hbm, gr_hbm, ur_hbm, gc_hbm, uc_hbm, acc, turned, cols, rows, gr, ur, gc, uc, load_sem, old_sem, z_send, y_send, k_send, x_send, z_recv, y_recv, k_recv, x_recv):
    n_row, n_z, n_y, n_k, width, splits, first, chunks = dims
    height, span = acc.shape
    tiles = span // width
    piece = rows.shape[3]
    thick = piece // splits
    together = n_y * n_k * piece
    r = lax.axis_index("row")
    c = lax.axis_index("col")
    k = lax.rem(c, n_k)
    y = lax.rem(c // n_k, n_y)
    z = c // (n_k * n_y)

    def at(z_, y_, k_):
        return (z_ * n_y + y_) * n_k + k_

    other_y = [lax.rem(y + 1, n_y)] if n_y > 1 else []
    other_k = [lax.rem(k + 1, n_k)] if n_k > 1 else []
    r_to = [lax.rem(r + d, n_row) for d in range(1, n_row)]
    r_from = [lax.rem(r + n_row - d, n_row) for d in range(1, n_row)]

    depth = gc.shape[0]
    head, tail = pl.ds(0, first), pl.ds(first, depth - first)
    col_loads = [[pltpu.make_async_copy(g.at[part], v.at[part], load_sem.at[2 * i + n]) for n, (g, v) in enumerate(((gc_hbm, gc), (uc_hbm, uc)))]
                 for i, part in enumerate((head, tail))]
    row_loads = [pltpu.make_async_copy(gr_hbm, gr, load_sem.at[4]), pltpu.make_async_copy(ur_hbm, ur, load_sem.at[5])]
    for load in col_loads[0] + row_loads:
        load.start()

    barrier = pltpu.get_barrier_semaphore()

    def greet(**device):
        pl.semaphore_signal(barrier, inc=1, device_id=device, device_id_type=MESH)

    for t in r_to:
        greet(row=t)
    for t in other_k:
        greet(col=at(z, y, t))
    for t in other_y:
        greet(col=at(z, t, k))
    if n_z > 1:
        @pl.when(z >= 1)
        def _():
            greet(col=at(z - 1, y, k))

        @pl.when(z + 1 < n_z)
        def _():
            greet(col=at(z + 1, y, k))
    if n_z > FAR:
        @pl.when(z == 0)
        def _():
            for t in range(FAR, n_z):
                greet(col=at(t, y, k))
    greetings = len(r_to) + len(other_k) + len(other_y) + jnp.where(z >= 1, 1, 0) + jnp.where(z + 1 < n_z, 1, 0) + jnp.where(z >= FAR, 1, 0)
    for load in col_loads[1]:
        load.start()
    old_load = pltpu.make_async_copy(old_hbm, acc, old_sem)

    def part_of(s, y_, k_, h):
        return rows.at[s, k_, y_, pl.ds(h * thick, thick)]

    def remote(ref, send_sem, recv_sem, **device):
        return pltpu.make_async_remote_copy(
            src_ref=ref, dst_ref=ref, send_sem=send_sem, recv_sem=recv_sem, device_id=device, device_id_type=MESH)

    def z_copy(s, h, way, t):
        return remote(part_of(s, y, k, h), z_send.at[way, s, h], z_recv.at[s, h], col=at(t, y, k))

    def y_copy(s, h):
        return remote(part_of(s, y, k, h), y_send, y_recv.at[s, h], col=at(z, other_y[0], k))

    def k_copy(s, y_, h):
        return remote(part_of(s, y_, k, h), k_send, k_recv.at[s], col=at(z, y, other_k[0]))

    def spread(s, h):
        if other_y:
            y_copy(s, h).start()
        if other_k:
            k_copy(s, y, h).start()

    def col_ref(s, chunk):
        j, start, size = chunk
        return cols.at[j, s, pl.ds(start, size)]

    def give_cols(chunk):
        j, start, size = chunk
        part, across = pl.ds(start, size), pl.ds(j * width, width)
        ref = col_ref(r, chunk)
        ref[...] = silu_product(gc[part, across], uc[part, across])
        if chunk is chunks[0]:
            pl.semaphore_wait(barrier, greetings)
        for i, t in enumerate(r_to):
            remote(ref, x_send.at[i], x_recv.at[r], row=t).start()

    for load in col_loads[0]:
        load.wait()
    give_cols(chunks[0])
    for load in row_loads:
        load.wait()
    rows[z, k, y] = silu_product(gr[...], ur[...])
    far = z >= FAR
    below = z >= 1
    above = z + 1 < n_z
    for h in range(splits):
        if n_z > FAR:
            pl.when(far)(lambda: z_copy(z, h, 2, 0).start())
        if n_z > 1:
            pl.when(below)(lambda: z_copy(z, h, 1, z - 1).start())
            pl.when(above)(lambda: z_copy(z, h, 0, z + 1).start())
        spread(z, h)
    for load in col_loads[1]:
        load.wait()
    for chunk in chunks[1:]:
        give_cols(chunk)
    old_load.start()

    def near(i):
        def key(a, s):
            return (1.5 if a == 0 and s >= FAR else abs(s - a), s > a, s)

        table = [sorted(range(n_z), key=functools.partial(key, a))[i] for a in range(n_z)]
        found = table[0]
        for a in range(1, n_z):
            found = jnp.where(z == a, table[a], found)
        return found

    def from_z(i, h):
        s = near(i)
        z_copy(s, h, 0, z).wait_recv()
        up = jnp.logical_and(s < z, above)
        down = jnp.logical_and(s > z, jnp.logical_or(z >= 2, jnp.logical_and(z == 1, s < FAR)))
        pl.when(up)(lambda: z_copy(s, h, 0, z + 1).start())
        pl.when(down)(lambda: z_copy(s, h, 1, z - 1).start())
        spread(s, h)

    def from_y(i, h):
        s = near(i)
        for t in other_y:
            remote(part_of(s, t, k, h), y_send, y_recv.at[s, h], col=c).wait_recv()
            for u in other_k:
                k_copy(s, t, h).start()

    def turn(i):
        s = near(i)
        for t in other_k:
            remote(rows.at[s, t], k_send, k_recv.at[s], col=c).wait_recv()
        parts = [rows[s, k_, y_] for y_ in range(n_y) for k_ in range(n_k)]
        turned[:, pl.ds(pl.multiple_of(s * together, together), together)] = jnp.concatenate(parts, axis=0).T

    halves = range(splits)
    for i in range(1, n_z):
        for h in halves:
            from_z(i, h)
        if i >= LAG:
            for h in halves:
                from_y(i - LAG, h)
    for i in range(max(n_z - LAG, 0), n_z):
        for h in halves:
            from_y(i, h)
    for i in range(n_z):
        turn(i)

    old_load.wait()
    for s in r_from:
        remote(cols.at[:, s], x_send.at[0], x_recv.at[s], row=r).wait_recv()
    for i, t in enumerate(r_to):
        remote(gc, x_send.at[i], x_recv.at[r], row=t).wait_send()
    if other_k:
        remote(rows.at[:, 0], k_send, k_recv.at[0], col=c).wait_send()
    if other_y:
        remote(rows.at[:, 0, 0], y_send, y_recv.at[0, 0], col=c).wait_send()
    for h in range(splits):
        for s in range(n_z if n_z > 1 else 0):
            up = jnp.logical_and(s <= z, above)
            down = jnp.logical_and(s >= z, jnp.logical_or(z >= 2, jnp.logical_and(z == 1, s == z if s >= FAR else True)))
            pl.when(up)(lambda: z_copy(s, h, 0, z).wait_send())
            pl.when(down)(lambda: z_copy(s, h, 1, z).wait_send())
        if n_z > FAR:
            pl.when(far)(lambda: z_copy(z, h, 2, 0).wait_send())


def finish_kernel(block, acc, turned, cols, out_hbm, out, sem):
    height, tokens = turned.shape
    tiles, width = cols.shape[0], cols.shape[3]
    stores = []
    for m in range(height // block):
        here = pl.ds(m * block, block)
        for j in range(tiles):
            there = pl.ds(j * width, width)
            out[here, there] = update(acc[here, there], turned[here], cols[j].reshape(tokens, width))
        stores.append(pltpu.make_async_copy(out.at[here], out_hbm.at[here], sem.at[m]))
        stores[-1].start()
    for store in stores:
        store.wait()


def cut(depth, parts):
    while parts > 1 and depth % (16 * parts):
        parts //= 2
    return depth // parts


def body(n_row, n_col, hessian_old, gate_rows, up_rows, gate_columns, up_columns):
    n_k = 2 if n_col % 2 == 0 else 1
    n_y = 2 if (n_col // n_k) % 2 == 0 else 1
    n_z = n_col // (n_k * n_y)
    height, span = hessian_old.shape
    piece = gate_rows.shape[0]
    depth = gate_columns.shape[0]
    width = 256 if span % 256 == 0 else span
    block = 128 if height % 128 == 0 else height
    tiles = span // width
    splits = piece // cut(piece, 2)
    first = cut(depth, 4)
    chunks = [(0, 0, first), (0, first, depth - first)] if first < depth else [(0, 0, depth)]
    chunks += [(j, 0, depth) for j in range(1, tiles)]
    inputs = (hessian_old, gate_rows, up_rows, gate_columns, up_columns)
    vmem = pl.BlockSpec(memory_space=pltpu.VMEM)
    hbm = pl.BlockSpec(memory_space=pltpu.HBM)
    gathered = pl.pallas_call(
        functools.partial(gather_kernel, (n_row, n_z, n_y, n_k, width, splits, first, chunks)),
        out_shape=(
            pltpu.VMEM((height, span), jnp.float32),
            pltpu.VMEM((height, n_col * piece), jnp.bfloat16),
            pltpu.VMEM((tiles, n_row, depth, width), jnp.bfloat16),
        ),
        in_specs=[hbm] * len(inputs),
        out_specs=(vmem, vmem, vmem),
        scratch_shapes=[
            pltpu.VMEM((n_z, n_k, n_y, piece, height), jnp.bfloat16),
            pltpu.VMEM((piece, height), jnp.bfloat16),
            pltpu.VMEM((piece, height), jnp.bfloat16),
            pltpu.VMEM((depth, span), jnp.bfloat16),
            pltpu.VMEM((depth, span), jnp.bfloat16),
            pltpu.SemaphoreType.DMA((6,)),
            pltpu.SemaphoreType.DMA,
            pltpu.SemaphoreType.DMA((3, n_z, splits)),
            pltpu.SemaphoreType.DMA,
            pltpu.SemaphoreType.DMA,
            pltpu.SemaphoreType.DMA((max(n_row - 1, 1),)),
            pltpu.SemaphoreType.DMA((n_z, splits)),
            pltpu.SemaphoreType.DMA((n_z, splits)),
            pltpu.SemaphoreType.DMA((n_z,)),
            pltpu.SemaphoreType.DMA((n_row,)),
        ],
        compiler_params=pltpu.CompilerParams(collective_id=0, has_side_effects=True, vmem_limit_bytes=LIMIT),
        name="gather",
    )(*(pltpu.with_memory_space_constraint(a, pltpu.HBM) for a in inputs))
    return pl.pallas_call(
        functools.partial(finish_kernel, block),
        out_shape=jax.ShapeDtypeStruct((height, span), jnp.float32),
        in_specs=[vmem] * 3,
        out_specs=hbm,
        scratch_shapes=[pltpu.VMEM((height, span), jnp.float32), pltpu.SemaphoreType.DMA((height // block,))],
        compiler_params=pltpu.CompilerParams(vmem_limit_bytes=LIMIT),
        name="finish",
    )(*gathered)


def solution(mesh):
    in_specs = (P("row", "col"), P("col", "row"), P("col", "row"), P("row", "col"), P("row", "col"))
    out_specs = P("row", "col")
    step = functools.partial(body, mesh.shape["row"], mesh.shape["col"])
    return jax.shard_map(step, mesh=mesh, in_specs=in_specs, out_specs=out_specs, check_vma=False)
```

```python
import functools

import jax
import jax.numpy as jnp
from jax import lax
from jax.experimental import pallas as pl
from jax.experimental.pallas import tpu as pltpu
from jax.sharding import PartitionSpec as P

MESH = pl.DeviceIdType.MESH
LIMIT = 40 * 1024 * 1024
FAR = 3
LAG = 2


def silu_product(gate, up):
    return (jax.nn.silu(gate.astype(jnp.float32)) * up.astype(jnp.float32)).astype(jnp.bfloat16)


def update(old, left, right):
    tokens = left.shape[1]
    total = jnp.dot(left, right, preferred_element_type=jnp.float32)
    total = total * (1.0 / tokens) if tokens & (tokens - 1) == 0 else total / tokens
    return 0.5 * old + total


def gather_kernel(dims, old_hbm, gr_hbm, ur_hbm, gc_hbm, uc_hbm, acc, turned, cols, rows, gr, ur, gc, uc, load_sem, old_sem, z_send, y_send, k_send, x_send, z_recv, y_recv, k_recv, x_recv):
    n_row, n_z, n_y, n_k, width, splits, first, chunks = dims
    height, span = acc.shape
    tiles = span // width
    piece = rows.shape[3]
    thick = piece // splits
    together = n_y * n_k * piece
    r = lax.axis_index("row")
    c = lax.axis_index("col")
    k = lax.rem(c, n_k)
    y = lax.rem(c // n_k, n_y)
    z = c // (n_k * n_y)

    def at(z_, y_, k_):
        return (z_ * n_y + y_) * n_k + k_

    other_y = [lax.rem(y + 1, n_y)] if n_y > 1 else []
    other_k = [lax.rem(k + 1, n_k)] if n_k > 1 else []
    r_to = [lax.rem(r + d, n_row) for d in range(1, n_row)]
    r_from = [lax.rem(r + n_row - d, n_row) for d in range(1, n_row)]

    depth = gc.shape[0]
    head, tail = pl.ds(0, first), pl.ds(first, depth - first)
    col_loads = [[pltpu.make_async_copy(g.at[part], v.at[part], load_sem.at[2 * i + n]) for n, (g, v) in enumerate(((gc_hbm, gc), (uc_hbm, uc)))]
                 for i, part in enumerate((head, tail))]
    row_loads = [pltpu.make_async_copy(gr_hbm, gr, load_sem.at[4]), pltpu.make_async_copy(ur_hbm, ur, load_sem.at[5])]

    barrier = pltpu.get_barrier_semaphore()

    def greet(**device):
        pl.semaphore_signal(barrier, inc=1, device_id=device, device_id_type=MESH)

    if n_z > 1:
        @pl.when(z >= 1)
        def _():
            greet(col=at(z - 1, y, k))

        @pl.when(z + 1 < n_z)
        def _():
            greet(col=at(z + 1, y, k))
    reach = jnp.where(k == 0, 2, FAR)
    for t in range(2, n_z):
        @pl.when(jnp.logical_and(z == 0, t >= reach))
        def _(t=t):
            greet(col=at(t, y, k))
    for t in other_y:
        greet(col=at(z, t, k))
    for t in r_to:
        greet(row=t)
    for t in other_k:
        greet(col=at(z, y, t))
    greetings = len(r_to) + len(other_k) + len(other_y) + jnp.where(z >= 1, 1, 0) + jnp.where(z + 1 < n_z, 1, 0) + jnp.where(z >= reach, 1, 0)
    for load in row_loads + col_loads[0] + col_loads[1]:
        load.start()
    old_load = pltpu.make_async_copy(old_hbm, acc, old_sem)

    def part_of(s, y_, k_, h):
        return rows.at[s, k_, y_, pl.ds(h * thick, thick)]

    def remote(ref, send_sem, recv_sem, **device):
        return pltpu.make_async_remote_copy(
            src_ref=ref, dst_ref=ref, send_sem=send_sem, recv_sem=recv_sem, device_id=device, device_id_type=MESH)

    def z_copy(s, h, way, t):
        return remote(part_of(s, y, k, h), z_send.at[way, s, h], z_recv.at[s, h], col=at(t, y, k))

    def y_copy(s, h):
        return remote(part_of(s, y, k, h), y_send, y_recv.at[s, h], col=at(z, other_y[0], k))

    def k_copy(s, y_, h):
        return remote(part_of(s, y_, k, h), k_send, k_recv.at[s], col=at(z, y, other_k[0]))

    def spread(s, h):
        if other_y:
            y_copy(s, h).start()
        if other_k:
            k_copy(s, y, h).start()

    def col_ref(s, chunk):
        j, start, size = chunk
        return cols.at[j, s, pl.ds(start, size)]

    def give_cols(chunk):
        j, start, size = chunk
        part, across = pl.ds(start, size), pl.ds(j * width, width)
        ref = col_ref(r, chunk)
        ref[...] = silu_product(gc[part, across], uc[part, across])
        for i, t in enumerate(r_to):
            remote(ref, x_send.at[i], x_recv.at[r], row=t).start()

    for load in row_loads:
        load.wait()
    rows[z, k, y] = silu_product(gr[...], ur[...])
    pl.semaphore_wait(barrier, greetings)
    far = z >= reach
    below = z >= 1
    above = z + 1 < n_z
    for h in range(splits):
        if n_z > 2:
            pl.when(far)(lambda: z_copy(z, h, 2, 0).start())
        if n_z > 1:
            pl.when(below)(lambda: z_copy(z, h, 1, z - 1).start())
            pl.when(above)(lambda: z_copy(z, h, 0, z + 1).start())
        spread(z, h)
    for load in col_loads[0]:
        load.wait()
    give_cols(chunks[0])
    for load in col_loads[1]:
        load.wait()
    for chunk in chunks[1:]:
        give_cols(chunk)
    old_load.start()

    def near(i):
        def key(a, s):
            return (1.5 if a == 0 and s >= FAR else abs(s - a), s > a, s)

        table = [sorted(range(n_z), key=functools.partial(key, a))[i] for a in range(n_z)]
        found = table[0]
        for a in range(1, n_z):
            found = jnp.where(z == a, table[a], found)
        return found

    def from_z(i, h):
        s = near(i)
        z_copy(s, h, 0, z).wait_recv()
        up = jnp.logical_and(s < z, above)
        down = jnp.logical_and(s > z, jnp.logical_or(z >= 2, jnp.logical_and(z == 1, s < reach)))
        pl.when(up)(lambda: z_copy(s, h, 0, z + 1).start())
        pl.when(down)(lambda: z_copy(s, h, 1, z - 1).start())
        spread(s, h)

    def from_y(i, h):
        s = near(i)
        for t in other_y:
            remote(part_of(s, t, k, h), y_send, y_recv.at[s, h], col=c).wait_recv()
            for u in other_k:
                k_copy(s, t, h).start()

    def turn(i):
        s = near(i)
        for t in other_k:
            remote(rows.at[s, t], k_send, k_recv.at[s], col=c).wait_recv()
        parts = [rows[s, k_, y_] for y_ in range(n_y) for k_ in range(n_k)]
        turned[:, pl.ds(pl.multiple_of(s * together, together), together)] = jnp.concatenate(parts, axis=0).T

    halves = range(splits)
    for i in range(1, n_z):
        for h in halves:
            from_z(i, h)
        if i >= LAG:
            for h in halves:
                from_y(i - LAG, h)
    for i in range(max(n_z - LAG, 0), n_z):
        for h in halves:
            from_y(i, h)
    for i in range(n_z):
        turn(i)

    old_load.wait()
    for s in r_from:
        remote(cols.at[:, s], x_send.at[0], x_recv.at[s], row=r).wait_recv()
    for i, t in enumerate(r_to):
        remote(gc, x_send.at[i], x_recv.at[r], row=t).wait_send()
    if other_k:
        remote(rows.at[:, 0], k_send, k_recv.at[0], col=c).wait_send()
    if other_y:
        remote(rows.at[:, 0, 0], y_send, y_recv.at[0, 0], col=c).wait_send()
    for h in range(splits):
        for s in range(n_z if n_z > 1 else 0):
            up = jnp.logical_and(s <= z, above)
            down = jnp.logical_and(s >= z, jnp.logical_or(z >= 2, jnp.logical_and(z == 1, jnp.logical_or(s == z, s < reach))))
            pl.when(up)(lambda: z_copy(s, h, 0, z).wait_send())
            pl.when(down)(lambda: z_copy(s, h, 1, z).wait_send())
        if n_z > 2:
            pl.when(far)(lambda: z_copy(z, h, 2, 0).wait_send())


def finish_kernel(block, acc, turned, cols, out_hbm, out, sem):
    height, tokens = turned.shape
    tiles, width = cols.shape[0], cols.shape[3]
    stores = []
    for m in range(height // block):
        here = pl.ds(m * block, block)
        for j in range(tiles):
            there = pl.ds(j * width, width)
            out[here, there] = update(acc[here, there], turned[here], cols[j].reshape(tokens, width))
        stores.append(pltpu.make_async_copy(out.at[here], out_hbm.at[here], sem.at[m]))
        stores[-1].start()
    for store in stores:
        store.wait()


def cut(depth, parts):
    while parts > 1 and depth % (16 * parts):
        parts //= 2
    return depth // parts


def body(n_row, n_col, hessian_old, gate_rows, up_rows, gate_columns, up_columns):
    n_k = 2 if n_col % 2 == 0 else 1
    n_y = 2 if (n_col // n_k) % 2 == 0 else 1
    n_z = n_col // (n_k * n_y)
    height, span = hessian_old.shape
    piece = gate_rows.shape[0]
    depth = gate_columns.shape[0]
    width = 256 if span % 256 == 0 else span
    block = 128 if height % 128 == 0 else height
    tiles = span // width
    splits = piece // cut(piece, 2)
    first = cut(depth, 4)
    chunks = [(0, 0, first), (0, first, depth - first)] if first < depth else [(0, 0, depth)]
    chunks += [(j, 0, depth) for j in range(1, tiles)]
    inputs = (hessian_old, gate_rows, up_rows, gate_columns, up_columns)
    vmem = pl.BlockSpec(memory_space=pltpu.VMEM)
    hbm = pl.BlockSpec(memory_space=pltpu.HBM)
    gathered = pl.pallas_call(
        functools.partial(gather_kernel, (n_row, n_z, n_y, n_k, width, splits, first, chunks)),
        out_shape=(
            pltpu.VMEM((height, span), jnp.float32),
            pltpu.VMEM((height, n_col * piece), jnp.bfloat16),
            pltpu.VMEM((tiles, n_row, depth, width), jnp.bfloat16),
        ),
        in_specs=[hbm] * len(inputs),
        out_specs=(vmem, vmem, vmem),
        scratch_shapes=[
            pltpu.VMEM((n_z, n_k, n_y, piece, height), jnp.bfloat16),
            pltpu.VMEM((piece, height), jnp.bfloat16),
            pltpu.VMEM((piece, height), jnp.bfloat16),
            pltpu.VMEM((depth, span), jnp.bfloat16),
            pltpu.VMEM((depth, span), jnp.bfloat16),
            pltpu.SemaphoreType.DMA((6,)),
            pltpu.SemaphoreType.DMA,
            pltpu.SemaphoreType.DMA((3, n_z, splits)),
            pltpu.SemaphoreType.DMA,
            pltpu.SemaphoreType.DMA,
            pltpu.SemaphoreType.DMA((max(n_row - 1, 1),)),
            pltpu.SemaphoreType.DMA((n_z, splits)),
            pltpu.SemaphoreType.DMA((n_z, splits)),
            pltpu.SemaphoreType.DMA((n_z,)),
            pltpu.SemaphoreType.DMA((n_row,)),
        ],
        compiler_params=pltpu.CompilerParams(collective_id=0, has_side_effects=True, vmem_limit_bytes=LIMIT),
        name="gather",
    )(*(pltpu.with_memory_space_constraint(a, pltpu.HBM) for a in inputs))
    return pl.pallas_call(
        functools.partial(finish_kernel, block),
        out_shape=jax.ShapeDtypeStruct((height, span), jnp.float32),
        in_specs=[vmem] * 3,
        out_specs=hbm,
        scratch_shapes=[pltpu.VMEM((height, span), jnp.float32), pltpu.SemaphoreType.DMA((height // block,))],
        compiler_params=pltpu.CompilerParams(vmem_limit_bytes=LIMIT),
        name="finish",
    )(*gathered)


def solution(mesh):
    in_specs = (P("row", "col"), P("col", "row"), P("col", "row"), P("row", "col"), P("row", "col"))
    out_specs = P("row", "col")
    step = functools.partial(body, mesh.shape["row"], mesh.shape["col"])
    return jax.shard_map(step, mesh=mesh, in_specs=in_specs, out_specs=out_specs, check_vma=False)
```
